32 devices in a mesh: fac: 2 (over core), str: 16 (over z, y, x).
Axes of the slice: x: 2, y: 2, z: 4, core: 2. Of those that a mesh axis runs over, the one named last changes fastest.
Arguments:
- vector: bfloat16 [4096, 8192], P('str'), may hold values from -6 to 6
- alpha_tiles: bfloat16 [2, 4, 128, 128], P('fac'), may hold values from -0.25 to 0.25
- alpha_pattern: int32 [2, 32, 4], P('fac'), may hold values from 0 to 31
- beta_tiles: bfloat16 [2, 4, 128, 128], P('fac'), may hold values from -0.25 to 0.25
- beta_pattern: int32 [2, 64, 4], P('fac'), may hold values from 0 to 63
- alpha_sector: int32 [32], replicated, may hold values from 0 to 1
- beta_sector: int32 [64], replicated, may hold values from 0 to 1
- alpha_diag: float32 [4096], replicated, may hold values from 0.5 to 2
- beta_diag: float32 [8192], replicated, may hold values from 0.5 to 2
- energy: float32 [1], replicated, may hold values from -1 to 0
Outputs:
- first_update: bfloat16 [4096, 8192], P('fac', 'str')
- second_update: bfloat16 [4096, 8192], P('str', 'fac')
The draws below stay inside these ranges and needn't reach their ends.
All inputs are finite; a program needn't handle non-finite values.
Results may differ from the reference program's by a relative error of at most 0.0064.
Values may be sent and summed in bfloat16 or wider, within the bound.
A program may use at most 128 MiB of HBM per device.

```python
import jax
import jax.numpy as jnp
from jax import lax

NA = 4096
NB = 8192
BLK = 128
S = 4
K = 2
NAB = 32
NBB = 64


def plant(values, key, smallest, high):
    place = [jax.random.randint(jax.random.fold_in(key, axis), (), 0, length) for axis, length in enumerate(values.shape)]
    widest = values.shape.index(max(values.shape))
    beside = place[:widest] + [(place[widest] + 1) % values.shape[widest]] + place[widest + 1:]
    return values.at[tuple(place)].set(smallest).at[tuple(beside)].set(high)


def steps_of(stream_key, dims, split, smallest, high):
    loudness, own = 1.0, jax.random.fold_in(stream_key, 6)
    for dim, parts in split:
        heights = jnp.exp(jax.random.uniform(jax.random.fold_in(own, dim), (parts,), jnp.float32, smallest / len(split), high / len(split)))
        loudness = loudness * jnp.repeat(heights, dims[dim] // parts).reshape([-1 if axis == dim else 1 for axis in range(len(dims))])
    return loudness


def scatter_about(own_key, shape, width, bound, cuts=(), kind=jnp.bfloat16):
    values = width * jax.random.normal(own_key, shape, jnp.float32)
    if cuts:
        values = values * steps_of(own_key, shape, cuts, -0.22, 0.18)
    return jnp.clip(values, -bound, bound).astype(kind)


def setup_inputs(seed: int = 0) -> dict:
    seeds = jax.random.split(jax.random.key(seed), 11)
    return {
        "vector": scatter_about(seeds[0], (NA, NB), 1.0, 6.0, ((0, 16),)),
        "alpha_tiles": scatter_about(seeds[1], (K, S, BLK, BLK), (BLK * S) ** -0.5, 0.25, ((0, 2),)),
        "alpha_pattern": plant(jax.random.randint(seeds[2], (K, NAB, S), 0, NAB), jax.random.fold_in(seeds[2], 1), 0, NAB - 1).astype(jnp.int32),
        "beta_tiles": scatter_about(seeds[3], (K, S, BLK, BLK), (BLK * S) ** -0.5, 0.25, ((0, 2),)),
        "beta_pattern": plant(jax.random.randint(seeds[4], (K, NBB, S), 0, NBB), jax.random.fold_in(seeds[4], 1), 0, NBB - 1).astype(jnp.int32),
        "alpha_sector": plant(jax.random.randint(seeds[5], (NAB,), 0, 2), jax.random.fold_in(seeds[5], 1), 0, 1).astype(jnp.int32),
        "beta_sector": plant(jax.random.randint(seeds[6], (NBB,), 0, 2), jax.random.fold_in(seeds[6], 1), 0, 1).astype(jnp.int32),
        "alpha_diag": jnp.clip(jax.random.uniform(seeds[7], (NA,), jnp.float32, 0.5, 2.0), 0.5, 2.0),
        "beta_diag": jnp.clip(jax.random.uniform(seeds[8], (NB,), jnp.float32, 0.5, 2.0), 0.5, 2.0),
        "energy": jnp.clip(jax.random.uniform(seeds[9], (1,), jnp.float32, -1.0, 0.0), -1.0, 0.0),
    }


def beta_apply(matrix, tile_set, pattern):
    height = matrix.shape[0]
    blocks = matrix.reshape(height, NBB, BLK).astype(jnp.float32)
    picked = jnp.take(blocks, pattern.reshape(-1), axis=1).reshape(height, NBB, S * BLK)
    stacked = tile_set.astype(jnp.float32).reshape(S * BLK, BLK)
    result = jnp.einsum("rjk,kc->rjc", picked, stacked)
    return result.reshape(height, NBB * BLK)


def alpha_apply(matrix, tile_set, pattern):
    breadth = matrix.shape[1]
    blocks = matrix.reshape(NAB, BLK, breadth).astype(jnp.float32)
    picked = jnp.take(blocks, pattern.reshape(-1), axis=0).reshape(NAB, S * BLK, breadth)
    stacked = tile_set.astype(jnp.float32).transpose(1, 0, 2).reshape(BLK, S * BLK)
    result = jnp.einsum("ak,jkc->jac", stacked, picked)
    return result.reshape(NAB * BLK, breadth)


def reference(vector, alpha_tiles, alpha_pattern, beta_tiles, beta_pattern, alpha_sector, beta_sector, alpha_diag, beta_diag, energy):
    live_mask = (jnp.repeat(alpha_sector, BLK)[:, None] == jnp.repeat(beta_sector, BLK)[None, :]).astype(jnp.float32)
    denominator = alpha_diag[:, None] + beta_diag[None, :] - energy[0]

    def forward(running, inputs):
        image = beta_apply(vector, inputs[2], inputs[3]).astype(jnp.bfloat16)
        return running + alpha_apply(image, inputs[0], inputs[1]), None

    factors = (alpha_tiles, alpha_pattern, beta_tiles, beta_pattern)
    sigma_first, _ = lax.scan(forward, jnp.zeros((NA, NB), jnp.float32), factors)
    first_update = (live_mask * sigma_first / denominator).astype(jnp.bfloat16)

    def backward(running, inputs):
        image = alpha_apply(first_update, inputs[0], inputs[1]).astype(jnp.bfloat16)
        return running + beta_apply(image, inputs[2], inputs[3]), None

    sigma_second, _ = lax.scan(backward, jnp.zeros((NA, NB), jnp.float32), factors)
    second_update = (live_mask * sigma_second / denominator).astype(jnp.bfloat16)
    return first_update, second_update
```

```python
import functools

import jax
import jax.numpy as jnp
from jax import lax
from jax.experimental import pallas as pl
from jax.experimental.pallas import tpu as pltpu
from jax.sharding import PartitionSpec as P

MESH = pl.DeviceIdType.MESH


def beta_apply(matrix, tile_set, pattern):
    height = matrix.shape[0]
    slot_count = tile_set.shape[0]
    block_size = tile_set.shape[1]
    count_blocks = matrix.shape[1] // block_size
    blocks = matrix.reshape(height, count_blocks, block_size)
    picked = jnp.take(blocks, pattern.reshape(-1), axis=1).reshape(
        height, count_blocks, slot_count * block_size
    )
    stacked = tile_set.reshape(slot_count * block_size, block_size)
    result = jnp.einsum("rjk,kc->rjc", picked, stacked, preferred_element_type=jnp.float32)
    return result.reshape(height, count_blocks * block_size)


def alpha_apply(matrix, tile_set, pattern):
    breadth = matrix.shape[1]
    slot_count = tile_set.shape[0]
    block_size = tile_set.shape[1]
    count_blocks = matrix.shape[0] // block_size
    blocks = matrix.reshape(count_blocks, block_size, breadth)
    picked = jnp.take(blocks, pattern.reshape(-1), axis=0).reshape(
        count_blocks, slot_count * block_size, breadth
    )
    stacked = tile_set.transpose(1, 0, 2).reshape(block_size, slot_count * block_size)
    result = jnp.einsum("ak,jkc->jac", stacked, picked, preferred_element_type=jnp.float32)
    return result.reshape(count_blocks * block_size, breadth)


def precondition(
    sigma_part,
    row_start,
    col_start,
    block_size,
    alpha_sector,
    beta_sector,
    alpha_diag,
    beta_diag,
    energy,
):
    row_count, col_count = sigma_part.shape
    row_blocks = row_count // block_size
    col_blocks = col_count // block_size
    alpha_labels = lax.dynamic_slice_in_dim(alpha_sector, row_start // block_size, row_blocks)
    beta_labels = lax.dynamic_slice_in_dim(beta_sector, col_start // block_size, col_blocks)
    live_mask = (alpha_labels[:, None, None, None] == beta_labels[None, None, :, None]).astype(
        jnp.float32
    )
    masked = (
        sigma_part.reshape(row_blocks, block_size, col_blocks, block_size) * live_mask
    ).reshape(row_count, col_count)
    alpha_part = lax.dynamic_slice_in_dim(alpha_diag, row_start, row_count)
    beta_part = lax.dynamic_slice_in_dim(beta_diag, col_start, col_count)
    denominator = alpha_part[:, None] + beta_part[None, :] - energy[0]
    return (masked / denominator).astype(jnp.bfloat16)


def body(
    vector,
    alpha_tiles,
    alpha_pattern,
    beta_tiles,
    beta_pattern,
    alpha_sector,
    beta_sector,
    alpha_diag,
    beta_diag,
    energy,
):
    string_index = lax.axis_index("str")
    group_index = lax.axis_index("fac")
    string_count = lax.axis_size("str")
    block_size = alpha_tiles.shape[2]
    row_count = vector.shape[0]
    col_count = vector.shape[1] // string_count
    factor = 0
    image = beta_apply(vector, beta_tiles[factor], beta_pattern[factor]).astype(jnp.bfloat16)
    moved_one = lax.all_to_all(image, "str", split_axis=1, concat_axis=0, tiled=True)
    partial_value = alpha_apply(moved_one, alpha_tiles[factor], alpha_pattern[factor])
    share_rows = lax.psum_scatter(partial_value, "fac", scatter_dimension=0, tiled=True)
    first_update = precondition(
        share_rows,
        group_index * share_rows.shape[0],
        string_index * col_count,
        block_size,
        alpha_sector,
        beta_sector,
        alpha_diag,
        beta_diag,
        energy,
    )
    whole_first = lax.all_gather(first_update, "fac", axis=0, tiled=True)
    factor = 0
    back_image = alpha_apply(whole_first, alpha_tiles[factor], alpha_pattern[factor]).astype(
        jnp.bfloat16
    )
    returned_one = lax.all_to_all(back_image, "str", split_axis=0, concat_axis=1, tiled=True)
    partial_back = beta_apply(returned_one, beta_tiles[factor], beta_pattern[factor])
    share_cols = lax.psum_scatter(partial_back, "fac", scatter_dimension=1, tiled=True)
    second_update = precondition(
        share_cols,
        string_index * row_count,
        group_index * share_cols.shape[1],
        block_size,
        alpha_sector,
        beta_sector,
        alpha_diag,
        beta_diag,
        energy,
    )
    return (first_update, second_update)


def exchange_kernel(
    sizes,
    vec,
    ta,
    tb,
    pa,
    pa_slot,
    pb,
    pb_slot,
    live,
    adiag,
    bdiag,
    energy,
    out1,
    out2,
    held,
    send1,
    recv1,
    first,
    send2,
    recv2,
    staged,
    send1_sem,
    recv1_sem,
    send2_sem,
    recv2_sem,
    o1_send,
    o1_recv,
    o2_send,
    o2_recv,
    held_sem,
):
    n, nf, bs, kc, sc, qc, nab, nbb = sizes
    me = lax.axis_index("str")
    c = lax.axis_index("fac")
    everyone = n * nf
    row_blocks = nab // n
    half_rows = nab // nf
    half_blocks = nbb // nf

    def partner(slot):
        return lax.rem(me + slot // nf, n), lax.rem(c + lax.rem(slot, nf), nf)

    def load(b, carry):
        columns = pl.ds(pl.multiple_of(b * bs, bs), bs)
        pltpu.make_async_copy(vec.at[:, columns], held.at[b], held_sem).start()
        return carry

    lax.fori_loop(0, nbb, load, 0)
    barrier = pltpu.get_barrier_semaphore()

    def greet(slot, carry):
        d, f = partner(slot)
        pl.semaphore_signal(
            barrier, inc=1, device_id={"fac": f, "str": d}, device_id_type=MESH
        )
        return carry

    lax.fori_loop(1, everyone, greet, 0)
    pl.semaphore_wait(barrier, everyone - 1)

    pltpu.make_async_copy(held, held, held_sem).wait()

    def column(ref, index):
        return jnp.transpose(jnp.broadcast_to(ref[pl.ds(index, 1), :], (bs, bs)))

    def beta_image(q, r, dst):
        d = lax.rem(me + r, n)
        j = (d * nf + c) * qc + q
        for k in range(kc):
            picked = jnp.concatenate(
                [
                    held[pb[(k * nbb + j) * sc + s]] for s in range(sc)
                ],
                axis=1,
            )
            image = jnp.dot(
                picked,
                tb[k * sc * bs : (k + 1) * sc * bs, :],
                preferred_element_type=jnp.float32,
            )
            for x in range(row_blocks):
                dst[x, k] = image[x * bs : (x + 1) * bs].astype(jnp.bfloat16)

    def first_slot(t):
        return 1 + lax.rem(t + n // 2 - 1, n - 1)

    def first_copy(q, t):
        r = first_slot(t)
        return pltpu.make_async_remote_copy(
            src_ref=send1[q].at[pl.ds(r * row_blocks, row_blocks)],
            dst_ref=recv1[q].at[pl.ds(r * row_blocks, row_blocks)],
            send_sem=send1_sem.at[q],
            recv_sem=recv1_sem.at[q],
            device_id={"fac": c, "str": lax.rem(me + r, n)},
            device_id_type=MESH,
        )

    for q in range(qc):

        def step_one(t, carry, q=q):
            r = first_slot(t)
            beta_image(q, r, send1[q].at[pl.ds(r * row_blocks, row_blocks)])

            @pl.when(t > 0)
            def _():
                first_copy(q, t - 1).start()

            return carry

        lax.fori_loop(0, n - 1, step_one, 0)
        beta_image(q, 0, recv1[q].at[pl.ds(0, row_blocks)])
        first_copy(q, n - 2).start()

    def second_slot(t):
        return 1 + lax.rem(t + everyone // 2 - 1, everyone - 1)

    def second_copy(q, t):
        slot = second_slot(t)
        d, f = partner(slot)
        return pltpu.make_async_remote_copy(
            src_ref=send2[q].at[slot],
            dst_ref=recv2.at[q * everyone + slot],
            send_sem=send2_sem.at[q],
            recv_sem=recv2_sem.at[q],
            device_id={"fac": f, "str": d},
            device_id_type=MESH,
        )

    def share_copy(q, e):
        f = lax.rem(c + e, nf)
        src = first[q].at[pl.ds(f * half_rows, half_rows)]
        dst = out1.at[:, :, pl.ds(pl.multiple_of((c * qc + q) * bs, bs), bs)]
        if e == 0:
            return pltpu.make_async_copy(src, dst, o1_send.at[q, e])
        return pltpu.make_async_remote_copy(
            src_ref=src,
            dst_ref=dst,
            send_sem=o1_send.at[q, e],
            recv_sem=o1_recv.at[q, e],
            device_id={"fac": f, "str": me},
            device_id_type=MESH,
        )

    for q in range(qc):
        landed = recv1[q].at[pl.ds(row_blocks, (n - 1) * row_blocks)]
        pltpu.make_async_copy(landed, landed, recv1_sem.at[q]).wait()
        j = (me * nf + c) * qc + q

        def sigma_one(i, carry, q=q, j=j):
            parts = []
            for k in range(kc):
                for s in range(sc):
                    parts.append(recv1[q][pa_slot[(k * nab + i) * sc + s], k])
            tiles = jnp.concatenate([ta[x] for x in range(kc * sc)], axis=1)
            sigma = jnp.dot(
                tiles, jnp.concatenate(parts, axis=0), preferred_element_type=jnp.float32
            )
            denominator = column(adiag, i) + bdiag[pl.ds(j, 1), :] - energy[0]
            value = (sigma * live[i * nbb + j] / denominator).astype(jnp.bfloat16)
            first[q][i] = value
            return carry

        lax.fori_loop(0, nab, sigma_one, 0)

        def alpha_image(slot, dst, q=q):
            d, f = partner(slot)
            i = d * nf + f
            for k in range(kc):
                picked = jnp.concatenate(
                    [
                        first[q][pa[(k * nab + i) * sc + s]] for s in range(sc)
                    ],
                    axis=0,
                )
                tiles = jnp.concatenate([ta[k * sc + s] for s in range(sc)], axis=1)
                image = jnp.dot(tiles, picked, preferred_element_type=jnp.float32)
                dst[k] = image.astype(jnp.bfloat16)

        def step_two(t, carry, q=q, alpha_image=alpha_image):
            slot = second_slot(t)
            alpha_image(slot, send2[q].at[slot])

            @pl.when(t > 0)
            def _():
                second_copy(q, t - 1).start()

            return carry

        lax.fori_loop(0, everyone - 1, step_two, 0)
        alpha_image(0, recv2.at[q * everyone])
        second_copy(q, everyone - 2).start()
        for e in range(nf):
            share_copy(q, e).start()

    for q in range(qc):
        landed = recv2.at[pl.ds(q * everyone + 1, everyone - 1)]
        pltpu.make_async_copy(landed, landed, recv2_sem.at[q]).wait()

    own = me * nf + c
    alpha_part = column(adiag, own)
    group = 4 if half_blocks % 4 == 0 else 1

    def sigma_two(first_block):
        rows = []
        for g in range(group):
            parts = []
            for k in range(kc):
                for s in range(sc):
                    slot = pb_slot[(k * nbb + first_block + g) * sc + s]
                    parts.append(recv2[slot, k])
            rows.append(jnp.concatenate(parts, axis=1))
        sigma = jnp.dot(
            jnp.concatenate(rows, axis=0), tb[...], preferred_element_type=jnp.float32
        )
        for g in range(group):
            j = first_block + g
            denominator = alpha_part + bdiag[pl.ds(j, 1), :] - energy[0]
            value = sigma[g * bs : (g + 1) * bs] * live[own * nbb + j] / denominator
            staged[:, pl.ds(pl.multiple_of(j * bs, bs), bs)] = value.astype(jnp.bfloat16)

    piece = group * (2 if half_blocks % (2 * group) == 0 else 1)
    pieces = half_blocks // piece

    def piece_copy(e, x):
        f = lax.rem(c + e, nf)
        src_start = pl.multiple_of((f * half_blocks + x * piece) * bs, bs)
        dst_start = pl.multiple_of(x * piece * bs, bs)
        src = staged.at[:, pl.ds(src_start, piece * bs)]
        dst = out2.at[pl.ds(pl.multiple_of(c * bs, bs), bs), pl.ds(dst_start, piece * bs)]
        if e == 0:
            return pltpu.make_async_copy(src, dst, o2_send.at[e])
        return pltpu.make_async_remote_copy(
            src_ref=src,
            dst_ref=dst,
            send_sem=o2_send.at[e],
            recv_sem=o2_recv.at[e],
            device_id={"fac": f, "str": me},
            device_id_type=MESH,
        )

    for e in reversed(range(nf)):

        def finish(x, carry, e=e):
            f = lax.rem(c + e, nf)
            for y in range(piece // group):
                sigma_two(f * half_blocks + x * piece + y * group)

            @pl.when(x > 0)
            def _():
                piece_copy(e, x - 1).start()

            return carry

        lax.fori_loop(0, pieces, finish, 0)
        piece_copy(e, pieces - 1).start()

    for q in range(qc):
        sent = send1[q].at[pl.ds(row_blocks, (n - 1) * row_blocks)]
        pltpu.make_async_copy(sent, sent, send1_sem.at[q]).wait()
        sent = send2[q].at[pl.ds(1, everyone - 1)]
        pltpu.make_async_copy(sent, sent, send2_sem.at[q]).wait()
        for e in range(nf):
            share_copy(q, e).wait()
    for e in range(nf):
        sent = staged.at[:, pl.ds(0, half_blocks * bs)]
        pltpu.make_async_copy(sent, sent, o2_send.at[e]).wait()
        if e > 0:
            pltpu.make_async_copy(sent, sent, o2_recv.at[e]).wait()


def gather_factors(value):
    count = lax.axis_size("fac")
    me = lax.axis_index("fac")
    shifted = [value]
    for step in range(1, count):
        pairs = [(x, (x + step) % count) for x in range(count)]
        shifted.append(lax.ppermute(value, "fac", pairs))
    whole = jnp.stack(shifted)
    order = lax.rem(me - jnp.arange(count) + count, count)
    return jnp.take(whole, order, axis=0)


def split_body(
    vector,
    alpha_tiles,
    alpha_pattern,
    beta_tiles,
    beta_pattern,
    alpha_sector,
    beta_sector,
    alpha_diag,
    beta_diag,
    energy,
):
    n = lax.axis_size("str")
    nf = lax.axis_size("fac")
    sc, bs = alpha_tiles.shape[1], alpha_tiles.shape[2]
    nab, nbb = alpha_sector.shape[0], beta_sector.shape[0]
    qc = nbb // (n * nf)
    kc = nf
    tiles = gather_factors(jnp.stack([alpha_tiles[0], beta_tiles[0]]))
    patterns = gather_factors(
        jnp.concatenate([alpha_pattern.reshape(-1), beta_pattern.reshape(-1)])
    )
    ta = tiles[:, 0].reshape(kc * sc, bs, bs)
    tb = tiles[:, 1].reshape(kc * sc * bs, bs)
    pa = patterns[:, : nab * sc].reshape(-1)
    pb = patterns[:, nab * sc :].reshape(-1)
    rows = vector.shape[0]
    me, c = lax.axis_index("str"), lax.axis_index("fac")
    row_blocks = nab // n
    pa_slot = lax.rem(me - pa // row_blocks + n, n) * row_blocks + lax.rem(pa, row_blocks)
    pb_slot = (
        lax.rem(pb, qc) * (n * nf)
        + lax.rem(me - pb // (nf * qc) + n, n) * nf
        + lax.rem(c - lax.rem(pb // qc, nf) + nf, nf)
    )
    live = (alpha_sector[:, None] == beta_sector[None, :]).astype(jnp.float32).reshape(-1)
    vmem = pl.BlockSpec(memory_space=pltpu.VMEM)
    smem = pl.BlockSpec(memory_space=pltpu.SMEM)
    anywhere = pl.BlockSpec(memory_space=pl.ANY)
    bf16 = jnp.bfloat16
    first_update, second_update = pl.pallas_call(
        functools.partial(exchange_kernel, (n, nf, bs, kc, sc, qc, nab, nbb)),
        out_shape=(
            jax.ShapeDtypeStruct((nab // nf, bs, nbb * bs // n), bf16),
            jax.ShapeDtypeStruct((rows, nbb * bs // nf), bf16),
        ),
        in_specs=[anywhere] + [vmem] * 2 + [smem] * 5 + [vmem] * 2 + [smem],
        out_specs=(anywhere, anywhere),
        scratch_shapes=[
            pltpu.VMEM((nbb, rows, bs), bf16),
            [pltpu.VMEM((nab, kc, bs, bs), bf16) for _ in range(qc)],
            [pltpu.VMEM((nab, kc, bs, bs), bf16) for _ in range(qc)],
            [pltpu.VMEM((nab, bs, bs), bf16) for _ in range(qc)],
            [pltpu.VMEM((n * nf, kc, bs, bs), bf16) for _ in range(qc)],
            pltpu.VMEM((qc * n * nf, kc, bs, bs), bf16),
            pltpu.VMEM((bs, nbb * bs), bf16),
            pltpu.SemaphoreType.DMA((qc,)),
            pltpu.SemaphoreType.DMA((qc,)),
            pltpu.SemaphoreType.DMA((qc,)),
            pltpu.SemaphoreType.DMA((qc,)),
            pltpu.SemaphoreType.DMA((qc, nf)),
            pltpu.SemaphoreType.DMA((qc, nf)),
            pltpu.SemaphoreType.DMA((nf,)),
            pltpu.SemaphoreType.DMA((nf,)),
            pltpu.SemaphoreType.DMA,
        ],
        compiler_params=pltpu.CompilerParams(
            collective_id=0, has_side_effects=True, vmem_limit_bytes=60 * 1024 * 1024
        ),
    )(
        vector,
        ta,
        tb,
        pa,
        pa_slot,
        pb,
        pb_slot,
        live,
        alpha_diag.reshape(nab, bs),
        beta_diag.reshape(nbb, bs),
        energy,
    )
    return first_update.reshape(nab * bs // nf, nbb * bs // n), second_update


def fits_split(*args):
    vector, alpha_tiles, _, _, _, alpha_sector, beta_sector = args[:7]
    n, nf = lax.axis_size("str"), lax.axis_size("fac")
    bs = alpha_tiles.shape[2]
    nab, nbb = alpha_sector.shape[0], beta_sector.shape[0]
    return (
        n > 1
        and nf > 1
        and alpha_tiles.shape[0] == 1
        and bs % 128 == 0
        and nab == n * nf
        and nbb % (n * nf) == 0
    )


def either_body(*args):
    return split_body(*args) if fits_split(*args) else body(*args)


def solution(mesh):
    return jax.shard_map(
        either_body,
        mesh=mesh,
        in_specs=(
            P("str", None),
            P("fac", None, None, None),
            P("fac", None, None),
            P("fac", None, None, None),
            P("fac", None, None),
            P(),
            P(),
            P(),
            P(),
            P(),
        ),
        out_specs=(P("fac", "str"), P("str", "fac")),
        check_vma=False,
    )
```

```python
import functools

import jax
import jax.numpy as jnp
from jax import lax
from jax.experimental import pallas as pl
from jax.experimental.pallas import tpu as pltpu
from jax.sharding import PartitionSpec as P

MESH = pl.DeviceIdType.MESH


def beta_apply(matrix, tile_set, pattern):
    height = matrix.shape[0]
    slot_count = tile_set.shape[0]
    block_size = tile_set.shape[1]
    count_blocks = matrix.shape[1] // block_size
    blocks = matrix.reshape(height, count_blocks, block_size)
    picked = jnp.take(blocks, pattern.reshape(-1), axis=1).reshape(
        height, count_blocks, slot_count * block_size
    )
    stacked = tile_set.reshape(slot_count * block_size, block_size)
    result = jnp.einsum("rjk,kc->rjc", picked, stacked, preferred_element_type=jnp.float32)
    return result.reshape(height, count_blocks * block_size)


def alpha_apply(matrix, tile_set, pattern):
    breadth = matrix.shape[1]
    slot_count = tile_set.shape[0]
    block_size = tile_set.shape[1]
    count_blocks = matrix.shape[0] // block_size
    blocks = matrix.reshape(count_blocks, block_size, breadth)
    picked = jnp.take(blocks, pattern.reshape(-1), axis=0).reshape(
        count_blocks, slot_count * block_size, breadth
    )
    stacked = tile_set.transpose(1, 0, 2).reshape(block_size, slot_count * block_size)
    result = jnp.einsum("ak,jkc->jac", stacked, picked, preferred_element_type=jnp.float32)
    return result.reshape(count_blocks * block_size, breadth)


def precondition(
    sigma_part,
    row_start,
    col_start,
    block_size,
    alpha_sector,
    beta_sector,
    alpha_diag,
    beta_diag,
    energy,
):
    row_count, col_count = sigma_part.shape
    row_blocks = row_count // block_size
    col_blocks = col_count // block_size
    alpha_labels = lax.dynamic_slice_in_dim(alpha_sector, row_start // block_size, row_blocks)
    beta_labels = lax.dynamic_slice_in_dim(beta_sector, col_start // block_size, col_blocks)
    live_mask = (alpha_labels[:, None, None, None] == beta_labels[None, None, :, None]).astype(
        jnp.float32
    )
    masked = (
        sigma_part.reshape(row_blocks, block_size, col_blocks, block_size) * live_mask
    ).reshape(row_count, col_count)
    alpha_part = lax.dynamic_slice_in_dim(alpha_diag, row_start, row_count)
    beta_part = lax.dynamic_slice_in_dim(beta_diag, col_start, col_count)
    denominator = alpha_part[:, None] + beta_part[None, :] - energy[0]
    return (masked / denominator).astype(jnp.bfloat16)


def body(
    vector,
    alpha_tiles,
    alpha_pattern,
    beta_tiles,
    beta_pattern,
    alpha_sector,
    beta_sector,
    alpha_diag,
    beta_diag,
    energy,
):
    string_index = lax.axis_index("str")
    group_index = lax.axis_index("fac")
    string_count = lax.axis_size("str")
    block_size = alpha_tiles.shape[2]
    row_count = vector.shape[0]
    col_count = vector.shape[1] // string_count
    factor = 0
    image = beta_apply(vector, beta_tiles[factor], beta_pattern[factor]).astype(jnp.bfloat16)
    moved_one = lax.all_to_all(image, "str", split_axis=1, concat_axis=0, tiled=True)
    partial_value = alpha_apply(moved_one, alpha_tiles[factor], alpha_pattern[factor])
    share_rows = lax.psum_scatter(partial_value, "fac", scatter_dimension=0, tiled=True)
    first_update = precondition(
        share_rows,
        group_index * share_rows.shape[0],
        string_index * col_count,
        block_size,
        alpha_sector,
        beta_sector,
        alpha_diag,
        beta_diag,
        energy,
    )
    whole_first = lax.all_gather(first_update, "fac", axis=0, tiled=True)
    factor = 0
    back_image = alpha_apply(whole_first, alpha_tiles[factor], alpha_pattern[factor]).astype(
        jnp.bfloat16
    )
    returned_one = lax.all_to_all(back_image, "str", split_axis=0, concat_axis=1, tiled=True)
    partial_back = beta_apply(returned_one, beta_tiles[factor], beta_pattern[factor])
    share_cols = lax.psum_scatter(partial_back, "fac", scatter_dimension=1, tiled=True)
    second_update = precondition(
        share_cols,
        string_index * row_count,
        group_index * share_cols.shape[1],
        block_size,
        alpha_sector,
        beta_sector,
        alpha_diag,
        beta_diag,
        energy,
    )
    return (first_update, second_update)


def exchange_kernel(
    sizes,
    vec,
    ta,
    tb,
    pa,
    pa_slot,
    pb,
    pb_slot,
    live,
    packed_rows,
    packed_slot,
    adiag,
    bdiag,
    energy,
    out1,
    out2,
    held,
    send1,
    recv1,
    first,
    packed,
    mirrored,
    expanded,
    send2,
    recv2,
    staged,
    send1_sem,
    recv1_sem,
    send2_sem,
    recv2_sem,
    mirror_send,
    mirror_recv,
    o1_send,
    o1_recv,
    o2_send,
    o2_recv,
    held_sem,
):
    n, nf, bs, kc, sc, qc, nab, nbb, cap = sizes
    hn = n // 2
    team = hn * nf
    me = lax.axis_index("str")
    c = lax.axis_index("fac")
    everyone = n * nf
    row_blocks = nab // n
    half_rows = nab // nf
    half_blocks = nbb // nf

    def partner(slot):
        return lax.rem(me + slot // nf, n), lax.rem(c + lax.rem(slot, nf), nf)

    def load(b, carry):
        columns = pl.ds(pl.multiple_of(b * bs, bs), bs)
        pltpu.make_async_copy(vec.at[:, columns], held.at[b], held_sem).start()
        return carry

    lax.fori_loop(0, nbb, load, 0)
    barrier = pltpu.get_barrier_semaphore()

    def greet(slot, carry):
        d, f = partner(slot)
        pl.semaphore_signal(
            barrier, inc=1, device_id={"fac": f, "str": d}, device_id_type=MESH
        )
        return carry

    lax.fori_loop(1, everyone, greet, 0)
    pl.semaphore_wait(barrier, everyone - 1)

    pltpu.make_async_copy(held, held, held_sem).wait()

    def column(ref, index):
        return jnp.transpose(jnp.broadcast_to(ref[pl.ds(index, 1), :], (bs, bs)))

    def beta_image(q, r, dst):
        d = lax.rem(me + r, n)
        j = (d * nf + c) * qc + q
        for k in range(kc):
            picked = jnp.concatenate(
                [
                    held[pb[(k * nbb + j) * sc + s]] for s in range(sc)
                ],
                axis=1,
            )
            image = jnp.dot(
                picked,
                tb[k * sc * bs : (k + 1) * sc * bs, :],
                preferred_element_type=jnp.float32,
            )
            for x in range(row_blocks):
                dst[x, k] = image[x * bs : (x + 1) * bs].astype(jnp.bfloat16)

    def first_slot(t):
        return 1 + lax.rem(t + n // 2 - 1, n - 1)

    def first_copy(q, t):
        r = first_slot(t)
        return pltpu.make_async_remote_copy(
            src_ref=send1[q].at[pl.ds(r * row_blocks, row_blocks)],
            dst_ref=recv1[q].at[pl.ds(r * row_blocks, row_blocks)],
            send_sem=send1_sem.at[q],
            recv_sem=recv1_sem.at[q],
            device_id={"fac": c, "str": lax.rem(me + r, n)},
            device_id_type=MESH,
        )

    for q in range(qc):

        def step_one(t, carry, q=q):
            r = first_slot(t)
            beta_image(q, r, send1[q].at[pl.ds(r * row_blocks, row_blocks)])

            @pl.when(t > 0)
            def _():
                first_copy(q, t - 1).start()

            return carry

        lax.fori_loop(0, n - 1, step_one, 0)
        beta_image(q, 0, recv1[q].at[pl.ds(0, row_blocks)])
        first_copy(q, n - 2).start()

    half, inside = me // hn, lax.rem(me, hn)
    mirror = lax.rem(me + hn, n)

    def teammate(slot):
        d = half * hn + lax.rem(inside + slot // nf, hn)
        return d, lax.rem(c + lax.rem(slot, nf), nf)

    def second_slot(t):
        return 1 + lax.rem(t + team // 2 - 1, team - 1)

    def second_copy(part, t):
        slot = second_slot(t)
        d, f = teammate(slot)
        return pltpu.make_async_remote_copy(
            src_ref=send2[part].at[slot],
            dst_ref=recv2.at[part * team + slot],
            send_sem=send2_sem.at[part],
            recv_sem=recv2_sem.at[part],
            device_id={"fac": f, "str": d},
            device_id_type=MESH,
        )

    def mirror_copy(q):
        return pltpu.make_async_remote_copy(
            src_ref=packed[q],
            dst_ref=mirrored[q],
            send_sem=mirror_send.at[q],
            recv_sem=mirror_recv.at[q],
            device_id={"fac": c, "str": mirror},
            device_id_type=MESH,
        )

    def spread_images(part, source):
        def alpha_image(slot, dst):
            d, f = teammate(slot)
            i = d * nf + f
            for k in range(kc):
                picked = jnp.concatenate(
                    [source[pa[(k * nab + i) * sc + s]] for s in range(sc)], axis=0
                )
                tiles = jnp.concatenate([ta[k * sc + s] for s in range(sc)], axis=1)
                image = jnp.dot(tiles, picked, preferred_element_type=jnp.float32)
                dst[k] = image.astype(jnp.bfloat16)

        def step_two(t, carry):
            slot = second_slot(t)
            alpha_image(slot, send2[part].at[slot])

            @pl.when(t > 0)
            def _():
                second_copy(part, t - 1).start()

            return carry

        lax.fori_loop(0, team - 1, step_two, 0)
        alpha_image(0, recv2.at[part * team])
        second_copy(part, team - 2).start()

    def share_copy(q, e):
        f = lax.rem(c + e, nf)
        src = first[q].at[pl.ds(f * half_rows, half_rows)]
        dst = out1.at[:, :, pl.ds(pl.multiple_of((c * qc + q) * bs, bs), bs)]
        if e == 0:
            return pltpu.make_async_copy(src, dst, o1_send.at[q, e])
        return pltpu.make_async_remote_copy(
            src_ref=src,
            dst_ref=dst,
            send_sem=o1_send.at[q, e],
            recv_sem=o1_recv.at[q, e],
            device_id={"fac": f, "str": me},
            device_id_type=MESH,
        )

    for q in range(qc):
        landed = recv1[q].at[pl.ds(row_blocks, (n - 1) * row_blocks)]
        pltpu.make_async_copy(landed, landed, recv1_sem.at[q]).wait()
        j = (me * nf + c) * qc + q

        def sigma_one(i, carry, q=q, j=j):
            parts = []
            for k in range(kc):
                for s in range(sc):
                    parts.append(recv1[q][pa_slot[(k * nab + i) * sc + s], k])
            tiles = jnp.concatenate([ta[x] for x in range(kc * sc)], axis=1)
            sigma = jnp.dot(
                tiles, jnp.concatenate(parts, axis=0), preferred_element_type=jnp.float32
            )
            denominator = column(adiag, i) + bdiag[pl.ds(j, 1), :] - energy[0]
            value = (sigma * live[i * nbb + j] / denominator).astype(jnp.bfloat16)
            first[q][i] = value
            return carry

        lax.fori_loop(0, nab, sigma_one, 0)

        def pack(x, carry, q=q, j=j):
            packed[q][x] = first[q][packed_rows[j * cap + x]]
            return carry

        lax.fori_loop(0, cap, pack, 0)
        mirror_copy(q).start()
        spread_images(2 * q, first[q])
        for e in range(nf):
            share_copy(q, e).start()

    for q in range(qc):
        mirror_copy(q).wait_recv()
        j = (mirror * nf + c) * qc + q

        def expand(i, carry, q=q, j=j):
            block = mirrored[q][packed_slot[j * nab + i]].astype(jnp.float32)
            expanded[q][i] = (block * live[i * nbb + j]).astype(jnp.bfloat16)
            return carry

        lax.fori_loop(0, nab, expand, 0)
        spread_images(2 * q + 1, expanded[q])

    for part in range(2 * qc):
        landed = recv2.at[pl.ds(part * team + 1, team - 1)]
        pltpu.make_async_copy(landed, landed, recv2_sem.at[part]).wait()

    own = me * nf + c
    alpha_part = column(adiag, own)
    group = 4 if half_blocks % 4 == 0 else 1

    def sigma_two(first_block):
        rows = []
        for g in range(group):
            parts = []
            for k in range(kc):
                for s in range(sc):
                    slot = pb_slot[(k * nbb + first_block + g) * sc + s]
                    parts.append(recv2[slot, k])
            rows.append(jnp.concatenate(parts, axis=1))
        sigma = jnp.dot(
            jnp.concatenate(rows, axis=0), tb[...], preferred_element_type=jnp.float32
        )
        for g in range(group):
            j = first_block + g
            denominator = alpha_part + bdiag[pl.ds(j, 1), :] - energy[0]
            value = sigma[g * bs : (g + 1) * bs] * live[own * nbb + j] / denominator
            staged[:, pl.ds(pl.multiple_of(j * bs, bs), bs)] = value.astype(jnp.bfloat16)

    piece = group * (2 if half_blocks % (2 * group) == 0 else 1)
    pieces = half_blocks // piece

    def piece_copy(e, x):
        f = lax.rem(c + e, nf)
        src_start = pl.multiple_of((f * half_blocks + x * piece) * bs, bs)
        dst_start = pl.multiple_of(x * piece * bs, bs)
        src = staged.at[:, pl.ds(src_start, piece * bs)]
        dst = out2.at[pl.ds(pl.multiple_of(c * bs, bs), bs), pl.ds(dst_start, piece * bs)]
        if e == 0:
            return pltpu.make_async_copy(src, dst, o2_send.at[e])
        return pltpu.make_async_remote_copy(
            src_ref=src,
            dst_ref=dst,
            send_sem=o2_send.at[e],
            recv_sem=o2_recv.at[e],
            device_id={"fac": f, "str": me},
            device_id_type=MESH,
        )

    for e in reversed(range(nf)):

        def finish(x, carry, e=e):
            f = lax.rem(c + e, nf)
            for y in range(piece // group):
                sigma_two(f * half_blocks + x * piece + y * group)

            @pl.when(x > 0)
            def _():
                piece_copy(e, x - 1).start()

            return carry

        lax.fori_loop(0, pieces, finish, 0)
        piece_copy(e, pieces - 1).start()

    for q in range(qc):
        sent = send1[q].at[pl.ds(row_blocks, (n - 1) * row_blocks)]
        pltpu.make_async_copy(sent, sent, send1_sem.at[q]).wait()
        for part in (2 * q, 2 * q + 1):
            sent = send2[part].at[pl.ds(1, team - 1)]
            pltpu.make_async_copy(sent, sent, send2_sem.at[part]).wait()
        mirror_copy(q).wait_send()
        for e in range(nf):
            share_copy(q, e).wait()
    for e in range(nf):
        sent = staged.at[:, pl.ds(0, half_blocks * bs)]
        pltpu.make_async_copy(sent, sent, o2_send.at[e]).wait()
        if e > 0:
            pltpu.make_async_copy(sent, sent, o2_recv.at[e]).wait()


def gather_factors(value):
    count = lax.axis_size("fac")
    me = lax.axis_index("fac")
    shifted = [value]
    for step in range(1, count):
        pairs = [(x, (x + step) % count) for x in range(count)]
        shifted.append(lax.ppermute(value, "fac", pairs))
    whole = jnp.stack(shifted)
    order = lax.rem(me - jnp.arange(count) + count, count)
    return jnp.take(whole, order, axis=0)


def split_body(
    vector,
    alpha_tiles,
    alpha_pattern,
    beta_tiles,
    beta_pattern,
    alpha_sector,
    beta_sector,
    alpha_diag,
    beta_diag,
    energy,
):
    n = lax.axis_size("str")
    nf = lax.axis_size("fac")
    sc, bs = alpha_tiles.shape[1], alpha_tiles.shape[2]
    nab, nbb = alpha_sector.shape[0], beta_sector.shape[0]
    qc = nbb // (n * nf)
    kc = nf
    tiles = gather_factors(jnp.stack([alpha_tiles[0], beta_tiles[0]]))
    patterns = gather_factors(
        jnp.concatenate([alpha_pattern.reshape(-1), beta_pattern.reshape(-1)])
    )
    ta = tiles[:, 0].reshape(kc * sc, bs, bs)
    tb = tiles[:, 1].reshape(kc * sc * bs, bs)
    pa = patterns[:, : nab * sc].reshape(-1)
    pb = patterns[:, nab * sc :].reshape(-1)
    rows = vector.shape[0]
    me, c = lax.axis_index("str"), lax.axis_index("fac")
    row_blocks = nab // n
    pa_slot = lax.rem(me - pa // row_blocks + n, n) * row_blocks + lax.rem(pa, row_blocks)
    hn = n // 2
    chip = pb // (nf * qc)
    crossed = (chip // hn != me // hn).astype(jnp.int32)
    pb_slot = (
        (lax.rem(pb, qc) * 2 + crossed) * (hn * nf)
        + lax.rem(me - chip + n, hn) * nf
        + lax.rem(c - lax.rem(pb // qc, nf) + nf, nf)
    )
    alive = alpha_sector[None, :] == beta_sector[:, None]
    live = alive.T.astype(jnp.float32).reshape(-1)
    index = jnp.arange(nab)
    place = jnp.sum(
        (alive[:, None, :] & (index[None, None, :] < index[None, :, None])).astype(jnp.int32),
        axis=2,
    )
    most = jnp.max(jnp.sum(alive.astype(jnp.int32), axis=1))
    vmem = pl.BlockSpec(memory_space=pltpu.VMEM)
    smem = pl.BlockSpec(memory_space=pltpu.SMEM)
    anywhere = pl.BlockSpec(memory_space=pl.ANY)
    bf16 = jnp.bfloat16
    call = lambda cap, rows_of, slot_of, ident: pl.pallas_call(
        functools.partial(exchange_kernel, (n, nf, bs, kc, sc, qc, nab, nbb, cap)),
        out_shape=(
            jax.ShapeDtypeStruct((nab // nf, bs, nbb * bs // n), bf16),
            jax.ShapeDtypeStruct((rows, nbb * bs // nf), bf16),
        ),
        in_specs=[anywhere] + [vmem] * 2 + [smem] * 7 + [vmem] * 2 + [smem],
        out_specs=(anywhere, anywhere),
        scratch_shapes=[
            pltpu.VMEM((nbb, rows, bs), bf16),
            [pltpu.VMEM((nab, kc, bs, bs), bf16) for _ in range(qc)],
            [pltpu.VMEM((nab, kc, bs, bs), bf16) for _ in range(qc)],
            [pltpu.VMEM((nab, bs, bs), bf16) for _ in range(qc)],
            [pltpu.VMEM((cap, bs, bs), bf16) for _ in range(qc)],
            [pltpu.VMEM((cap, bs, bs), bf16) for _ in range(qc)],
            [pltpu.VMEM((nab, bs, bs), bf16) for _ in range(qc)],
            [pltpu.VMEM((n // 2 * nf, kc, bs, bs), bf16) for _ in range(2 * qc)],
            pltpu.VMEM((qc * n * nf, kc, bs, bs), bf16),
            pltpu.VMEM((bs, nbb * bs), bf16),
            pltpu.SemaphoreType.DMA((qc,)),
            pltpu.SemaphoreType.DMA((qc,)),
            pltpu.SemaphoreType.DMA((2 * qc,)),
            pltpu.SemaphoreType.DMA((2 * qc,)),
            pltpu.SemaphoreType.DMA((qc,)),
            pltpu.SemaphoreType.DMA((qc,)),
            pltpu.SemaphoreType.DMA((qc, nf)),
            pltpu.SemaphoreType.DMA((qc, nf)),
            pltpu.SemaphoreType.DMA((nf,)),
            pltpu.SemaphoreType.DMA((nf,)),
            pltpu.SemaphoreType.DMA,
        ],
        compiler_params=pltpu.CompilerParams(
            collective_id=ident, has_side_effects=True, vmem_limit_bytes=60 * 1024 * 1024
        ),
    )(
        vector,
        ta,
        tb,
        pa,
        pa_slot,
        pb,
        pb_slot,
        live,
        rows_of,
        slot_of,
        alpha_diag.reshape(nab, bs),
        beta_diag.reshape(nbb, bs),
        energy,
    )

    def with_room(cap, ident):
        chosen = alive[:, None, :] & (place[:, None, :] == jnp.arange(cap)[None, :, None])
        rows_of = jnp.sum(jnp.where(chosen, index[None, None, :], 0), axis=2).reshape(-1)
        slot_of = jnp.where(alive, place, 0).reshape(-1)
        return call(cap, rows_of, slot_of, ident)

    room = nab * 11 // 16
    first_update, second_update = lax.cond(
        most <= room, lambda: with_room(room, 0), lambda: with_room(nab, 1)
    )
    return first_update.reshape(nab * bs // nf, nbb * bs // n), second_update


def fits_split(*args):
    vector, alpha_tiles, _, _, _, alpha_sector, beta_sector = args[:7]
    n, nf = lax.axis_size("str"), lax.axis_size("fac")
    bs = alpha_tiles.shape[2]
    nab, nbb = alpha_sector.shape[0], beta_sector.shape[0]
    return (
        n > 2
        and n % 2 == 0
        and nf > 1
        and alpha_tiles.shape[0] == 1
        and bs % 128 == 0
        and nab == n * nf
        and nbb % (n * nf) == 0
    )


def either_body(*args):
    return split_body(*args) if fits_split(*args) else body(*args)


def solution(mesh):
    return jax.shard_map(
        either_body,
        mesh=mesh,
        in_specs=(
            P("str", None),
            P("fac", None, None, None),
            P("fac", None, None),
            P("fac", None, None, None),
            P("fac", None, None),
            P(),
            P(),
            P(),
            P(),
            P(),
        ),
        out_specs=(P("fac", "str"), P("str", "fac")),
        check_vma=False,
    )
```

```python
import functools

import jax
import jax.numpy as jnp
from jax import lax
from jax.experimental import pallas as pl
from jax.experimental.pallas import tpu as pltpu
from jax.sharding import PartitionSpec as P

MESH = pl.DeviceIdType.MESH


def beta_apply(matrix, tile_set, pattern):
    height = matrix.shape[0]
    slot_count = tile_set.shape[0]
    block_size = tile_set.shape[1]
    count_blocks = matrix.shape[1] // block_size
    blocks = matrix.reshape(height, count_blocks, block_size)
    picked = jnp.take(blocks, pattern.reshape(-1), axis=1).reshape(
        height, count_blocks, slot_count * block_size
    )
    stacked = tile_set.reshape(slot_count * block_size, block_size)
    result = jnp.einsum("rjk,kc->rjc", picked, stacked, preferred_element_type=jnp.float32)
    return result.reshape(height, count_blocks * block_size)


def alpha_apply(matrix, tile_set, pattern):
    breadth = matrix.shape[1]
    slot_count = tile_set.shape[0]
    block_size = tile_set.shape[1]
    count_blocks = matrix.shape[0] // block_size
    blocks = matrix.reshape(count_blocks, block_size, breadth)
    picked = jnp.take(blocks, pattern.reshape(-1), axis=0).reshape(
        count_blocks, slot_count * block_size, breadth
    )
    stacked = tile_set.transpose(1, 0, 2).reshape(block_size, slot_count * block_size)
    result = jnp.einsum("ak,jkc->jac", stacked, picked, preferred_element_type=jnp.float32)
    return result.reshape(count_blocks * block_size, breadth)


def precondition(
    sigma_part,
    row_start,
    col_start,
    block_size,
    alpha_sector,
    beta_sector,
    alpha_diag,
    beta_diag,
    energy,
):
    row_count, col_count = sigma_part.shape
    row_blocks = row_count // block_size
    col_blocks = col_count // block_size
    alpha_labels = lax.dynamic_slice_in_dim(alpha_sector, row_start // block_size, row_blocks)
    beta_labels = lax.dynamic_slice_in_dim(beta_sector, col_start // block_size, col_blocks)
    live_mask = (alpha_labels[:, None, None, None] == beta_labels[None, None, :, None]).astype(
        jnp.float32
    )
    masked = (
        sigma_part.reshape(row_blocks, block_size, col_blocks, block_size) * live_mask
    ).reshape(row_count, col_count)
    alpha_part = lax.dynamic_slice_in_dim(alpha_diag, row_start, row_count)
    beta_part = lax.dynamic_slice_in_dim(beta_diag, col_start, col_count)
    denominator = alpha_part[:, None] + beta_part[None, :] - energy[0]
    return (masked / denominator).astype(jnp.bfloat16)


def body(
    vector,
    alpha_tiles,
    alpha_pattern,
    beta_tiles,
    beta_pattern,
    alpha_sector,
    beta_sector,
    alpha_diag,
    beta_diag,
    energy,
):
    string_index = lax.axis_index("str")
    group_index = lax.axis_index("fac")
    string_count = lax.axis_size("str")
    block_size = alpha_tiles.shape[2]
    row_count = vector.shape[0]
    col_count = vector.shape[1] // string_count
    factor = 0
    image = beta_apply(vector, beta_tiles[factor], beta_pattern[factor]).astype(jnp.bfloat16)
    moved_one = lax.all_to_all(image, "str", split_axis=1, concat_axis=0, tiled=True)
    partial_value = alpha_apply(moved_one, alpha_tiles[factor], alpha_pattern[factor])
    share_rows = lax.psum_scatter(partial_value, "fac", scatter_dimension=0, tiled=True)
    first_update = precondition(
        share_rows,
        group_index * share_rows.shape[0],
        string_index * col_count,
        block_size,
        alpha_sector,
        beta_sector,
        alpha_diag,
        beta_diag,
        energy,
    )
    whole_first = lax.all_gather(first_update, "fac", axis=0, tiled=True)
    factor = 0
    back_image = alpha_apply(whole_first, alpha_tiles[factor], alpha_pattern[factor]).astype(
        jnp.bfloat16
    )
    returned_one = lax.all_to_all(back_image, "str", split_axis=0, concat_axis=1, tiled=True)
    partial_back = beta_apply(returned_one, beta_tiles[factor], beta_pattern[factor])
    share_cols = lax.psum_scatter(partial_back, "fac", scatter_dimension=1, tiled=True)
    second_update = precondition(
        share_cols,
        string_index * row_count,
        group_index * share_cols.shape[1],
        block_size,
        alpha_sector,
        beta_sector,
        alpha_diag,
        beta_diag,
        energy,
    )
    return (first_update, second_update)


def exchange_kernel(
    sizes,
    vec,
    ta,
    tb,
    pa,
    pa_slot,
    pb,
    pb_slot,
    live,
    adiag,
    bdiag,
    energy,
    out1,
    out2,
    held,
    send1,
    recv1,
    first,
    send2,
    recv2,
    staged,
    send1_sem,
    recv1_sem,
    send2_sem,
    recv2_sem,
    o1_send,
    o1_recv,
    o2_send,
    o2_recv,
    held_sem,
):
    n, nf, bs, kc, sc, qc, nab, nbb = sizes
    me = lax.axis_index("str")
    c = lax.axis_index("fac")
    everyone = n * nf
    row_blocks = nab // n
    half_rows = nab // nf
    half_blocks = nbb // nf

    def factor_of(k):
        return lax.rem(c - k + nf, nf)

    def partner(slot):
        return lax.rem(me + slot // nf, n), lax.rem(c + lax.rem(slot, nf), nf)

    def load(b, carry):
        columns = pl.ds(pl.multiple_of(b * bs, bs), bs)
        pltpu.make_async_copy(vec.at[:, columns], held.at[b], held_sem).start()
        return carry

    lax.fori_loop(0, nbb, load, 0)
    barrier = pltpu.get_barrier_semaphore()

    def greet(slot, carry):
        d, f = partner(slot)
        pl.semaphore_signal(
            barrier, inc=1, device_id={"fac": f, "str": d}, device_id_type=MESH
        )
        return carry

    lax.fori_loop(1, everyone, greet, 0)
    pl.semaphore_wait(barrier, everyone - 1)

    pltpu.make_async_copy(held, held, held_sem).wait()

    def column(ref, index):
        return jnp.transpose(jnp.broadcast_to(ref[pl.ds(index, 1), :], (bs, bs)))

    def beta_image(q, r, dst):
        d = lax.rem(me + r, n)
        j = (d * nf + c) * qc + q
        for k in range(kc):
            picked = jnp.concatenate(
                [
                    held[pb[(k * nbb + j) * sc + s]] for s in range(sc)
                ],
                axis=1,
            )
            image = jnp.dot(
                picked,
                tb[k][...],
                preferred_element_type=jnp.float32,
            )
            for x in range(row_blocks):
                dst[x, k] = image[x * bs : (x + 1) * bs].astype(jnp.bfloat16)

    def first_slot(t):
        return 1 + lax.rem(t + n // 2 - 1, n - 1)

    def first_copy(q, t):
        r = first_slot(t)
        return pltpu.make_async_remote_copy(
            src_ref=send1[q].at[pl.ds(r * row_blocks, row_blocks)],
            dst_ref=recv1[q].at[pl.ds(r * row_blocks, row_blocks)],
            send_sem=send1_sem.at[q],
            recv_sem=recv1_sem.at[q],
            device_id={"fac": c, "str": lax.rem(me + r, n)},
            device_id_type=MESH,
        )

    for q in range(qc):

        def step_one(t, carry, q=q):
            r = first_slot(t)
            beta_image(q, r, send1[q].at[pl.ds(r * row_blocks, row_blocks)])

            @pl.when(t > 0)
            def _():
                first_copy(q, t - 1).start()

            return carry

        lax.fori_loop(0, n - 1, step_one, 0)
        beta_image(q, 0, recv1[q].at[pl.ds(0, row_blocks)])
        first_copy(q, n - 2).start()

    def second_slot(t):
        return 1 + lax.rem(t + everyone // 2 - 1, everyone - 1)

    def second_copy(q, t):
        slot = second_slot(t)
        d, f = partner(slot)
        return pltpu.make_async_remote_copy(
            src_ref=send2[q].at[slot],
            dst_ref=recv2.at[q * everyone + slot],
            send_sem=send2_sem.at[q],
            recv_sem=recv2_sem.at[q],
            device_id={"fac": f, "str": d},
            device_id_type=MESH,
        )

    def share_copy(q, e):
        f = lax.rem(c + e, nf)
        src = first[q].at[pl.ds(f * half_rows, half_rows)]
        dst = out1.at[:, :, pl.ds(pl.multiple_of((c * qc + q) * bs, bs), bs)]
        if e == 0:
            return pltpu.make_async_copy(src, dst, o1_send.at[q, e])
        return pltpu.make_async_remote_copy(
            src_ref=src,
            dst_ref=dst,
            send_sem=o1_send.at[q, e],
            recv_sem=o1_recv.at[q, e],
            device_id={"fac": f, "str": me},
            device_id_type=MESH,
        )

    for q in range(qc):
        landed = recv1[q].at[pl.ds(row_blocks, (n - 1) * row_blocks)]
        pltpu.make_async_copy(landed, landed, recv1_sem.at[q]).wait()
        j = (me * nf + c) * qc + q

        def sigma_one(i, carry, q=q, j=j):
            parts = []
            for k in range(kc):
                for s in range(sc):
                    parts.append(recv1[q][pa_slot[(k * nab + i) * sc + s], k])
            tiles = jnp.concatenate([ta[k][s] for k in range(kc) for s in range(sc)], axis=1)
            sigma = jnp.dot(
                tiles, jnp.concatenate(parts, axis=0), preferred_element_type=jnp.float32
            )
            denominator = column(adiag, i) + bdiag[pl.ds(j, 1), :] - energy[0]
            value = (sigma * live[i * nbb + j] / denominator).astype(jnp.bfloat16)
            first[q][i] = value
            return carry

        lax.fori_loop(0, nab, sigma_one, 0)

        def alpha_image(slot, dst, q=q):
            d, f = partner(slot)
            i = d * nf + f
            for k in range(kc):
                picked = jnp.concatenate(
                    [
                        first[q][pa[(k * nab + i) * sc + s]] for s in range(sc)
                    ],
                    axis=0,
                )
                tiles = jnp.concatenate([ta[k][s] for s in range(sc)], axis=1)
                image = jnp.dot(tiles, picked, preferred_element_type=jnp.float32)
                dst[factor_of(k)] = image.astype(jnp.bfloat16)

        def step_two(t, carry, q=q, alpha_image=alpha_image):
            slot = second_slot(t)
            alpha_image(slot, send2[q].at[slot])

            @pl.when(t > 0)
            def _():
                second_copy(q, t - 1).start()

            return carry

        lax.fori_loop(0, everyone - 1, step_two, 0)
        alpha_image(0, recv2.at[q * everyone])
        second_copy(q, everyone - 2).start()
        for e in range(nf):
            share_copy(q, e).start()

    for q in range(qc):
        landed = recv2.at[pl.ds(q * everyone + 1, everyone - 1)]
        pltpu.make_async_copy(landed, landed, recv2_sem.at[q]).wait()

    own = me * nf + c
    alpha_part = column(adiag, own)
    group = 4 if half_blocks % 4 == 0 else 1

    def sigma_two(first_block):
        stacked = jnp.concatenate([tb[k][...] for k in range(kc)], axis=0)
        rows = []
        for g in range(group):
            parts = []
            for k in range(kc):
                for s in range(sc):
                    slot = pb_slot[(k * nbb + first_block + g) * sc + s]
                    parts.append(recv2[slot, factor_of(k)])
            rows.append(jnp.concatenate(parts, axis=1))
        sigma = jnp.dot(
            jnp.concatenate(rows, axis=0), stacked, preferred_element_type=jnp.float32
        )
        for g in range(group):
            j = first_block + g
            denominator = alpha_part + bdiag[pl.ds(j, 1), :] - energy[0]
            value = sigma[g * bs : (g + 1) * bs] * live[own * nbb + j] / denominator
            staged[:, pl.ds(pl.multiple_of(j * bs, bs), bs)] = value.astype(jnp.bfloat16)

    piece = group * (2 if half_blocks % (2 * group) == 0 else 1)
    pieces = half_blocks // piece

    def piece_copy(e, x):
        f = lax.rem(c + e, nf)
        src_start = pl.multiple_of((f * half_blocks + x * piece) * bs, bs)
        dst_start = pl.multiple_of(x * piece * bs, bs)
        src = staged.at[:, pl.ds(src_start, piece * bs)]
        dst = out2.at[pl.ds(pl.multiple_of(c * bs, bs), bs), pl.ds(dst_start, piece * bs)]
        if e == 0:
            return pltpu.make_async_copy(src, dst, o2_send.at[e])
        return pltpu.make_async_remote_copy(
            src_ref=src,
            dst_ref=dst,
            send_sem=o2_send.at[e],
            recv_sem=o2_recv.at[e],
            device_id={"fac": f, "str": me},
            device_id_type=MESH,
        )

    for e in reversed(range(nf)):

        def finish(x, carry, e=e):
            f = lax.rem(c + e, nf)
            for y in range(piece // group):
                sigma_two(f * half_blocks + x * piece + y * group)

            @pl.when(x > 0)
            def _():
                piece_copy(e, x - 1).start()

            return carry

        lax.fori_loop(0, pieces, finish, 0)
        piece_copy(e, pieces - 1).start()

    for q in range(qc):
        sent = send1[q].at[pl.ds(row_blocks, (n - 1) * row_blocks)]
        pltpu.make_async_copy(sent, sent, send1_sem.at[q]).wait()
        sent = send2[q].at[pl.ds(1, everyone - 1)]
        pltpu.make_async_copy(sent, sent, send2_sem.at[q]).wait()
        for e in range(nf):
            share_copy(q, e).wait()
    for e in range(nf):
        sent = staged.at[:, pl.ds(0, half_blocks * bs)]
        pltpu.make_async_copy(sent, sent, o2_send.at[e]).wait()
        if e > 0:
            pltpu.make_async_copy(sent, sent, o2_recv.at[e]).wait()


def gather_factors(value):
    count = lax.axis_size("fac")
    me = lax.axis_index("fac")
    shifted = [value]
    for step in range(1, count):
        pairs = [(x, (x + step) % count) for x in range(count)]
        shifted.append(lax.ppermute(value, "fac", pairs))
    return shifted


def split_body(
    vector,
    alpha_tiles,
    alpha_pattern,
    beta_tiles,
    beta_pattern,
    alpha_sector,
    beta_sector,
    alpha_diag,
    beta_diag,
    energy,
):
    n = lax.axis_size("str")
    nf = lax.axis_size("fac")
    sc, bs = alpha_tiles.shape[1], alpha_tiles.shape[2]
    nab, nbb = alpha_sector.shape[0], beta_sector.shape[0]
    qc = nbb // (n * nf)
    kc = nf
    ta = gather_factors(alpha_tiles[0])
    tb = [x.reshape(sc * bs, bs) for x in gather_factors(beta_tiles[0])]
    patterns = jnp.stack(gather_factors(
        jnp.concatenate([alpha_pattern.reshape(-1), beta_pattern.reshape(-1)])
    ))
    pa = patterns[:, : nab * sc].reshape(-1)
    pb = patterns[:, nab * sc :].reshape(-1)
    rows = vector.shape[0]
    me, c = lax.axis_index("str"), lax.axis_index("fac")
    row_blocks = nab // n
    pa_slot = lax.rem(me - pa // row_blocks + n, n) * row_blocks + lax.rem(pa, row_blocks)
    pb_slot = (
        lax.rem(pb, qc) * (n * nf)
        + lax.rem(me - pb // (nf * qc) + n, n) * nf
        + lax.rem(c - lax.rem(pb // qc, nf) + nf, nf)
    )
    live = (alpha_sector[:, None] == beta_sector[None, :]).astype(jnp.float32).reshape(-1)
    vmem = pl.BlockSpec(memory_space=pltpu.VMEM)
    smem = pl.BlockSpec(memory_space=pltpu.SMEM)
    anywhere = pl.BlockSpec(memory_space=pl.ANY)
    bf16 = jnp.bfloat16
    first_update, second_update = pl.pallas_call(
        functools.partial(exchange_kernel, (n, nf, bs, kc, sc, qc, nab, nbb)),
        out_shape=(
            jax.ShapeDtypeStruct((nab // nf, bs, nbb * bs // n), bf16),
            jax.ShapeDtypeStruct((rows, nbb * bs // nf), bf16),
        ),
        in_specs=[anywhere, [vmem] * nf, [vmem] * nf] + [smem] * 5 + [vmem] * 2 + [smem],
        out_specs=(anywhere, anywhere),
        scratch_shapes=[
            pltpu.VMEM((nbb, rows, bs), bf16),
            [pltpu.VMEM((nab, kc, bs, bs), bf16) for _ in range(qc)],
            [pltpu.VMEM((nab, kc, bs, bs), bf16) for _ in range(qc)],
            [pltpu.VMEM((nab, bs, bs), bf16) for _ in range(qc)],
            [pltpu.VMEM((n * nf, kc, bs, bs), bf16) for _ in range(qc)],
            pltpu.VMEM((qc * n * nf, kc, bs, bs), bf16),
            pltpu.VMEM((bs, nbb * bs), bf16),
            pltpu.SemaphoreType.DMA((qc,)),
            pltpu.SemaphoreType.DMA((qc,)),
            pltpu.SemaphoreType.DMA((qc,)),
            pltpu.SemaphoreType.DMA((qc,)),
            pltpu.SemaphoreType.DMA((qc, nf)),
            pltpu.SemaphoreType.DMA((qc, nf)),
            pltpu.SemaphoreType.DMA((nf,)),
            pltpu.SemaphoreType.DMA((nf,)),
            pltpu.SemaphoreType.DMA,
        ],
        compiler_params=pltpu.CompilerParams(
            collective_id=0, has_side_effects=True, vmem_limit_bytes=60 * 1024 * 1024
        ),
    )(
        vector,
        ta,
        tb,
        pa,
        pa_slot,
        pb,
        pb_slot,
        live,
        alpha_diag.reshape(nab, bs),
        beta_diag.reshape(nbb, bs),
        energy,
    )
    return first_update.reshape(nab * bs // nf, nbb * bs // n), second_update


def fits_split(*args):
    vector, alpha_tiles, _, _, _, alpha_sector, beta_sector = args[:7]
    n, nf = lax.axis_size("str"), lax.axis_size("fac")
    bs = alpha_tiles.shape[2]
    nab, nbb = alpha_sector.shape[0], beta_sector.shape[0]
    return (
        n > 1
        and nf > 1
        and alpha_tiles.shape[0] == 1
        and bs % 128 == 0
        and nab == n * nf
        and nbb % (n * nf) == 0
    )


def either_body(*args):
    return split_body(*args) if fits_split(*args) else body(*args)


def solution(mesh):
    return jax.shard_map(
        either_body,
        mesh=mesh,
        in_specs=(
            P("str", None),
            P("fac", None, None, None),
            P("fac", None, None),
            P("fac", None, None, None),
            P("fac", None, None),
            P(),
            P(),
            P(),
            P(),
            P(),
        ),
        out_specs=(P("fac", "str"), P("str", "fac")),
        check_vma=False,
    )
```

```python
import functools

import jax
import jax.numpy as jnp
from jax import lax
from jax.experimental import pallas as pl
from jax.experimental.pallas import tpu as pltpu
from jax.sharding import PartitionSpec as P

MESH = pl.DeviceIdType.MESH


def beta_apply(matrix, tile_set, pattern):
    height = matrix.shape[0]
    slot_count = tile_set.shape[0]
    block_size = tile_set.shape[1]
    count_blocks = matrix.shape[1] // block_size
    blocks = matrix.reshape(height, count_blocks, block_size)
    picked = jnp.take(blocks, pattern.reshape(-1), axis=1).reshape(
        height, count_blocks, slot_count * block_size
    )
    stacked = tile_set.reshape(slot_count * block_size, block_size)
    result = jnp.einsum("rjk,kc->rjc", picked, stacked, preferred_element_type=jnp.float32)
    return result.reshape(height, count_blocks * block_size)


def alpha_apply(matrix, tile_set, pattern):
    breadth = matrix.shape[1]
    slot_count = tile_set.shape[0]
    block_size = tile_set.shape[1]
    count_blocks = matrix.shape[0] // block_size
    blocks = matrix.reshape(count_blocks, block_size, breadth)
    picked = jnp.take(blocks, pattern.reshape(-1), axis=0).reshape(
        count_blocks, slot_count * block_size, breadth
    )
    stacked = tile_set.transpose(1, 0, 2).reshape(block_size, slot_count * block_size)
    result = jnp.einsum("ak,jkc->jac", stacked, picked, preferred_element_type=jnp.float32)
    return result.reshape(count_blocks * block_size, breadth)


def precondition(
    sigma_part,
    row_start,
    col_start,
    block_size,
    alpha_sector,
    beta_sector,
    alpha_diag,
    beta_diag,
    energy,
):
    row_count, col_count = sigma_part.shape
    row_blocks = row_count // block_size
    col_blocks = col_count // block_size
    alpha_labels = lax.dynamic_slice_in_dim(alpha_sector, row_start // block_size, row_blocks)
    beta_labels = lax.dynamic_slice_in_dim(beta_sector, col_start // block_size, col_blocks)
    live_mask = (alpha_labels[:, None, None, None] == beta_labels[None, None, :, None]).astype(
        jnp.float32
    )
    masked = (
        sigma_part.reshape(row_blocks, block_size, col_blocks, block_size) * live_mask
    ).reshape(row_count, col_count)
    alpha_part = lax.dynamic_slice_in_dim(alpha_diag, row_start, row_count)
    beta_part = lax.dynamic_slice_in_dim(beta_diag, col_start, col_count)
    denominator = alpha_part[:, None] + beta_part[None, :] - energy[0]
    return (masked / denominator).astype(jnp.bfloat16)


def body(
    vector,
    alpha_tiles,
    alpha_pattern,
    beta_tiles,
    beta_pattern,
    alpha_sector,
    beta_sector,
    alpha_diag,
    beta_diag,
    energy,
):
    string_index = lax.axis_index("str")
    group_index = lax.axis_index("fac")
    string_count = lax.axis_size("str")
    block_size = alpha_tiles.shape[2]
    row_count = vector.shape[0]
    col_count = vector.shape[1] // string_count
    factor = 0
    image = beta_apply(vector, beta_tiles[factor], beta_pattern[factor]).astype(jnp.bfloat16)
    moved_one = lax.all_to_all(image, "str", split_axis=1, concat_axis=0, tiled=True)
    partial_value = alpha_apply(moved_one, alpha_tiles[factor], alpha_pattern[factor])
    share_rows = lax.psum_scatter(partial_value, "fac", scatter_dimension=0, tiled=True)
    first_update = precondition(
        share_rows,
        group_index * share_rows.shape[0],
        string_index * col_count,
        block_size,
        alpha_sector,
        beta_sector,
        alpha_diag,
        beta_diag,
        energy,
    )
    whole_first = lax.all_gather(first_update, "fac", axis=0, tiled=True)
    factor = 0
    back_image = alpha_apply(whole_first, alpha_tiles[factor], alpha_pattern[factor]).astype(
        jnp.bfloat16
    )
    returned_one = lax.all_to_all(back_image, "str", split_axis=0, concat_axis=1, tiled=True)
    partial_back = beta_apply(returned_one, beta_tiles[factor], beta_pattern[factor])
    share_cols = lax.psum_scatter(partial_back, "fac", scatter_dimension=1, tiled=True)
    second_update = precondition(
        share_cols,
        string_index * row_count,
        group_index * share_cols.shape[1],
        block_size,
        alpha_sector,
        beta_sector,
        alpha_diag,
        beta_diag,
        energy,
    )
    return (first_update, second_update)


def exchange_kernel(
    sizes,
    vec,
    ta,
    tb,
    pa,
    pa_slot,
    pb,
    pb_slot,
    live,
    adiag,
    bdiag,
    energy,
    out1,
    out2,
    held,
    send1,
    recv1,
    first,
    send2,
    recv2,
    staged,
    send1_sem,
    recv1_sem,
    send2_sem,
    recv2_sem,
    o1_send,
    o1_recv,
    o2_send,
    o2_recv,
    held_sem,
):
    n, nf, bs, kc, sc, qc, nab, nbb = sizes
    me = lax.axis_index("str")
    c = lax.axis_index("fac")
    everyone = n * nf
    row_blocks = nab // n
    half_rows = nab // nf
    half_blocks = nbb // nf

    def factor_of(k):
        return lax.rem(c - k + nf, nf)

    def partner(slot):
        return lax.rem(me + slot // nf, n), lax.rem(c + lax.rem(slot, nf), nf)

    def load(b, carry):
        columns = pl.ds(pl.multiple_of(b * bs, bs), bs)
        pltpu.make_async_copy(vec.at[:, columns], held.at[b], held_sem).start()
        return carry

    lax.fori_loop(0, nbb, load, 0)
    barrier = pltpu.get_barrier_semaphore()

    def greet(slot, carry):
        d, f = partner(slot)
        pl.semaphore_signal(
            barrier, inc=1, device_id={"fac": f, "str": d}, device_id_type=MESH
        )
        return carry

    lax.fori_loop(1, everyone, greet, 0)
    pl.semaphore_wait(barrier, everyone - 1)

    pltpu.make_async_copy(held, held, held_sem).wait()

    def column(ref, index):
        return jnp.transpose(jnp.broadcast_to(ref[pl.ds(index, 1), :], (bs, bs)))

    def beta_image(q, r, dst):
        d = lax.rem(me + r, n)
        j = (d * nf + c) * qc + q
        for k in range(kc):
            picked = jnp.concatenate(
                [
                    held[pb[(k * nbb + j) * sc + s]] for s in range(sc)
                ],
                axis=1,
            )
            image = jnp.dot(
                picked,
                tb[k][...],
                preferred_element_type=jnp.float32,
            )
            for x in range(row_blocks):
                dst[x, k] = image[x * bs : (x + 1) * bs].astype(jnp.bfloat16)

    def first_slot(t):
        return 1 + lax.rem(t + n // 2 - 1, n - 1)

    def first_copy(q, t):
        r = first_slot(t)
        return pltpu.make_async_remote_copy(
            src_ref=send1[q].at[pl.ds(r * row_blocks, row_blocks)],
            dst_ref=recv1[q].at[pl.ds(r * row_blocks, row_blocks)],
            send_sem=send1_sem.at[q],
            recv_sem=recv1_sem.at[q],
            device_id={"fac": c, "str": lax.rem(me + r, n)},
            device_id_type=MESH,
        )

    for q in range(qc):

        def step_one(t, carry, q=q):
            r = first_slot(t)
            beta_image(q, r, send1[q].at[pl.ds(r * row_blocks, row_blocks)])

            @pl.when(t > 0)
            def _():
                first_copy(q, t - 1).start()

            return carry

        lax.fori_loop(0, n - 1, step_one, 0)
        beta_image(q, 0, recv1[q].at[pl.ds(0, row_blocks)])
        first_copy(q, n - 2).start()

    def second_slot(t):
        return 1 + lax.rem(t + everyone // 2 - 1, everyone - 1)

    def second_copy(q, t):
        slot = second_slot(t)
        d, f = partner(slot)
        return pltpu.make_async_remote_copy(
            src_ref=send2[q].at[slot],
            dst_ref=recv2.at[q * everyone + slot],
            send_sem=send2_sem.at[q],
            recv_sem=recv2_sem.at[q],
            device_id={"fac": f, "str": d},
            device_id_type=MESH,
        )

    def share_copy(q, e):
        f = lax.rem(c + e, nf)
        src = first[q].at[pl.ds(f * half_rows, half_rows)]
        dst = out1.at[:, :, pl.ds(pl.multiple_of((c * qc + q) * bs, bs), bs)]
        if e == 0:
            return pltpu.make_async_copy(src, dst, o1_send.at[q, e])
        return pltpu.make_async_remote_copy(
            src_ref=src,
            dst_ref=dst,
            send_sem=o1_send.at[q, e],
            recv_sem=o1_recv.at[q, e],
            device_id={"fac": f, "str": me},
            device_id_type=MESH,
        )

    for q in range(qc):
        landed = recv1[q].at[pl.ds(row_blocks, (n - 1) * row_blocks)]
        pltpu.make_async_copy(landed, landed, recv1_sem.at[q]).wait()
        j = (me * nf + c) * qc + q

        def sigma_one(i, carry, q=q, j=j):
            parts = []
            for k in range(kc):
                for s in range(sc):
                    parts.append(recv1[q][pa_slot[(k * nab + i) * sc + s], k])
            tiles = jnp.concatenate([ta[k][s] for k in range(kc) for s in range(sc)], axis=1)
            sigma = jnp.dot(
                tiles, jnp.concatenate(parts, axis=0), preferred_element_type=jnp.float32
            )
            denominator = column(adiag, i) + bdiag[pl.ds(j, 1), :] - energy[0]
            value = (sigma * live[i * nbb + j] / denominator).astype(jnp.bfloat16)
            first[q][i] = value
            return carry

        lax.fori_loop(0, nab, sigma_one, 0)

        def alpha_image(slot, dst, q=q):
            d, f = partner(slot)
            i = d * nf + f
            for k in range(kc):
                picked = jnp.concatenate(
                    [
                        first[q][pa[(k * nab + i) * sc + s]] for s in range(sc)
                    ],
                    axis=0,
                )
                tiles = jnp.concatenate([ta[k][s] for s in range(sc)], axis=1)
                image = jnp.dot(tiles, picked, preferred_element_type=jnp.float32)
                dst[factor_of(k)] = image.astype(jnp.bfloat16)

        def step_two(t, carry, q=q, alpha_image=alpha_image):
            slot = second_slot(t)
            alpha_image(slot, send2[q].at[slot])

            @pl.when(t > 0)
            def _():
                second_copy(q, t - 1).start()

            return carry

        lax.fori_loop(0, everyone - 1, step_two, 0)
        alpha_image(0, recv2.at[q * everyone])
        second_copy(q, everyone - 2).start()
        for e in range(nf):
            share_copy(q, e).start()

    for q in range(qc):
        landed = recv2.at[pl.ds(q * everyone + 1, everyone - 1)]
        pltpu.make_async_copy(landed, landed, recv2_sem.at[q]).wait()

    own = me * nf + c
    alpha_part = column(adiag, own)
    group = 4 if half_blocks % 4 == 0 else 1

    def sigma_two(first_block):
        stacked = jnp.concatenate([tb[k][...] for k in range(kc)], axis=0)
        rows = []
        for g in range(group):
            parts = []
            for k in range(kc):
                for s in range(sc):
                    slot = pb_slot[(k * nbb + first_block + g) * sc + s]
                    parts.append(recv2[slot, factor_of(k)])
            rows.append(jnp.concatenate(parts, axis=1))
        sigma = jnp.dot(
            jnp.concatenate(rows, axis=0), stacked, preferred_element_type=jnp.float32
        )
        for g in range(group):
            j = first_block + g
            denominator = alpha_part + bdiag[pl.ds(j, 1), :] - energy[0]
            value = sigma[g * bs : (g + 1) * bs] * live[own * nbb + j] / denominator
            staged[:, pl.ds(pl.multiple_of(j * bs, bs), bs)] = value.astype(jnp.bfloat16)

    piece = group * (2 if half_blocks % (2 * group) == 0 else 1)
    pieces = half_blocks // piece

    def piece_copy(e, x):
        f = lax.rem(c + e, nf)
        src_start = pl.multiple_of((f * half_blocks + x * piece) * bs, bs)
        dst_start = pl.multiple_of(x * piece * bs, bs)
        src = staged.at[:, pl.ds(src_start, piece * bs)]
        dst = out2.at[pl.ds(pl.multiple_of(c * bs, bs), bs), pl.ds(dst_start, piece * bs)]
        if e == 0:
            return pltpu.make_async_copy(src, dst, o2_send.at[e])
        return pltpu.make_async_remote_copy(
            src_ref=src,
            dst_ref=dst,
            send_sem=o2_send.at[e],
            recv_sem=o2_recv.at[e],
            device_id={"fac": f, "str": me},
            device_id_type=MESH,
        )

    for e in reversed(range(nf)):

        def finish(x, carry, e=e):
            f = lax.rem(c + e, nf)
            for y in range(piece // group):
                sigma_two(f * half_blocks + x * piece + y * group)

            @pl.when(x > 0)
            def _():
                piece_copy(e, x - 1).start()

            return carry

        lax.fori_loop(0, pieces, finish, 0)
        piece_copy(e, pieces - 1).start()

    for q in range(qc):
        sent = send1[q].at[pl.ds(row_blocks, (n - 1) * row_blocks)]
        pltpu.make_async_copy(sent, sent, send1_sem.at[q]).wait()
        sent = send2[q].at[pl.ds(1, everyone - 1)]
        pltpu.make_async_copy(sent, sent, send2_sem.at[q]).wait()
        for e in range(nf):
            share_copy(q, e).wait()
    for e in range(nf):
        sent = staged.at[:, pl.ds(0, half_blocks * bs)]
        pltpu.make_async_copy(sent, sent, o2_send.at[e]).wait()
        if e > 0:
            pltpu.make_async_copy(sent, sent, o2_recv.at[e]).wait()


def gather_factors(value):
    count = lax.axis_size("fac")
    me = lax.axis_index("fac")
    shifted = [value]
    for step in range(1, count):
        pairs = [(x, (x + step) % count) for x in range(count)]
        shifted.append(lax.ppermute(value, "fac", pairs))
    return shifted


def split_body(
    vector,
    alpha_tiles,
    alpha_pattern,
    beta_tiles,
    beta_pattern,
    alpha_sector,
    beta_sector,
    alpha_diag,
    beta_diag,
    energy,
):
    n = lax.axis_size("str")
    nf = lax.axis_size("fac")
    sc, bs = alpha_tiles.shape[1], alpha_tiles.shape[2]
    nab, nbb = alpha_sector.shape[0], beta_sector.shape[0]
    qc = nbb // (n * nf)
    kc = nf
    ta = gather_factors(alpha_tiles[0])
    tb = [x.reshape(sc * bs, bs) for x in gather_factors(beta_tiles[0])]
    patterns = jnp.stack(gather_factors(
        jnp.concatenate([alpha_pattern.reshape(-1), beta_pattern.reshape(-1)])
    ))
    pa = patterns[:, : nab * sc].reshape(-1)
    pb = patterns[:, nab * sc :].reshape(-1)
    rows = vector.shape[0]
    me, c = lax.axis_index("str"), lax.axis_index("fac")
    row_blocks = nab // n
    pa_slot = lax.rem(me - pa // row_blocks + n, n) * row_blocks + lax.rem(pa, row_blocks)
    pb_slot = (
        lax.rem(pb, qc) * (n * nf)
        + lax.rem(me - pb // (nf * qc) + n, n) * nf
        + lax.rem(c - lax.rem(pb // qc, nf) + nf, nf)
    )
    live = (alpha_sector[:, None] == beta_sector[None, :]).astype(jnp.float32).reshape(-1)
    vmem = pl.BlockSpec(memory_space=pltpu.VMEM)
    smem = pl.BlockSpec(memory_space=pltpu.SMEM)
    anywhere = pl.BlockSpec(memory_space=pl.ANY)
    bf16 = jnp.bfloat16
    first_update, second_update = pl.pallas_call(
        functools.partial(exchange_kernel, (n, nf, bs, kc, sc, qc, nab, nbb)),
        out_shape=(
            jax.ShapeDtypeStruct((nab // nf, bs, nbb * bs // n), bf16),
            jax.ShapeDtypeStruct((rows, nbb * bs // nf), bf16),
        ),
        in_specs=[anywhere, [vmem] * nf, [vmem] * nf] + [smem] * 5 + [vmem] * 2 + [smem],
        out_specs=(anywhere, anywhere),
        scratch_shapes=[
            pltpu.VMEM((nbb, rows, bs), bf16),
            [pltpu.VMEM((nab, kc, bs, bs), bf16) for _ in range(qc)],
            [pltpu.VMEM((nab, kc, bs, bs), bf16) for _ in range(qc)],
            [pltpu.VMEM((nab, bs, bs), bf16) for _ in range(qc)],
            [pltpu.VMEM((n * nf, kc, bs, bs), bf16) for _ in range(qc)],
            pltpu.VMEM((qc * n * nf, kc, bs, bs), bf16),
            pltpu.VMEM((bs, nbb * bs), bf16),
            pltpu.SemaphoreType.DMA((qc,)),
            pltpu.SemaphoreType.DMA((qc,)),
            pltpu.SemaphoreType.DMA((qc,)),
            pltpu.SemaphoreType.DMA((qc,)),
            pltpu.SemaphoreType.DMA((qc, nf)),
            pltpu.SemaphoreType.DMA((qc, nf)),
            pltpu.SemaphoreType.DMA((nf,)),
            pltpu.SemaphoreType.DMA((nf,)),
            pltpu.SemaphoreType.DMA,
        ],
        compiler_params=pltpu.CompilerParams(
            collective_id=0, has_side_effects=True, vmem_limit_bytes=32 * 1024 * 1024
        ),
    )(
        vector,
        ta,
        tb,
        pa,
        pa_slot,
        pb,
        pb_slot,
        live,
        alpha_diag.reshape(nab, bs),
        beta_diag.reshape(nbb, bs),
        energy,
    )
    return first_update.reshape(nab * bs // nf, nbb * bs // n), second_update


def fits_split(*args):
    vector, alpha_tiles, _, _, _, alpha_sector, beta_sector = args[:7]
    n, nf = lax.axis_size("str"), lax.axis_size("fac")
    bs = alpha_tiles.shape[2]
    nab, nbb = alpha_sector.shape[0], beta_sector.shape[0]
    return (
        n > 1
        and nf > 1
        and alpha_tiles.shape[0] == 1
        and bs % 128 == 0
        and nab == n * nf
        and nbb % (n * nf) == 0
    )


def either_body(*args):
    return split_body(*args) if fits_split(*args) else body(*args)


def solution(mesh):
    return jax.shard_map(
        either_body,
        mesh=mesh,
        in_specs=(
            P("str", None),
            P("fac", None, None, None),
            P("fac", None, None),
            P("fac", None, None, None),
            P("fac", None, None),
            P(),
            P(),
            P(),
            P(),
            P(),
        ),
        out_specs=(P("fac", "str"), P("str", "fac")),
        check_vma=False,
    )
```
